256 devices in a mesh: cluster: 64 (over x, z, core), tile: 4 (over y).
Axes of the slice: x: 4, y: 4, z: 8, core: 2. Of those that a mesh axis runs over, the one named last changes fastest.
Arguments:
- points: bfloat16 [512, 8, 512], P('cluster', None, 'tile'), as said below
- charges: bfloat16 [512, 512, 256], P('cluster', 'tile'), may hold values from -6 to 6
- near_ids: int32 [512, 8], P('cluster'), may hold values from 0 to 511, as said below
- near_count: int32 [512], P('cluster'), may hold values from 1 to 8, as said below
- leaf_pivots: int32 [512, 256], P('cluster'), may hold values from 0 to 511, as said below
- merge_pivots: int32 [256, 6, 256], P('cluster'), may hold values from 0 to 511, as said below
Outputs:
- near_field: bfloat16 [512, 512, 256], P('cluster', 'tile')
- top_weights: bfloat16 [64, 256, 256], P('cluster', None, 'tile')
The draws below stay inside these ranges and needn't reach their ends.
Inputs may be any that keep to these rules, and one draw needn't show every extreme that they name: `near_ids`: slot 0 of box b holds b itself and slots from near_count[b] on repeat b; the other used slots name distinct boxes other than b at most 4 boxes away from b; some box names a box exactly 4 away. `near_count`: some box uses all 8 slots. `leaf_pivots`: the pivots of a box are distinct. `merge_pivots`: the pivots of a row are distinct; rows q and q2 of level l are equal when q // 2^l == q2 // 2^l. The points of a box lie around a centre that moves along a smooth curve with the box number.
All inputs are finite; a program needn't handle non-finite values.
Results may differ from the reference program's by a relative error of at most 0.005.
Values may be sent and summed in bfloat16 or wider, within the bound.
A program may use at most 192 MiB of HBM per device.

```python
import jax
import jax.numpy as jnp
from jax import lax

FEAT = 8
LEAF = 512
RANK = 256
R = 256
LEAF_DEV = 8
LEVELS = 6
MOST = 8
SPAN = 4
BOXES = 512
N_CLUSTER = 64


def draw_points(key, part):
    shape = (BOXES, FEAT, LEAF)
    key_phase, key_spread = jax.random.split(jax.random.fold_in(key, 3))
    phases = jax.random.uniform(key_phase, (FEAT,), jnp.float32, -3.1, 3.1)
    rates = 0.02 + 0.004 * jnp.arange(FEAT).astype(jnp.float32)
    box_numbers = jnp.arange(BOXES).astype(jnp.float32)
    centres = 4.0 * jnp.sin(box_numbers[:, None] * rates[None, :] + phases[None, :])
    spread = 0.3 * jax.random.truncated_normal(key_spread, -4.0, 4.0, shape, jnp.float32)
    values = centres[:, :, None] + spread
    return values.astype(jnp.bfloat16)


def near_lists(key):
    base_key = jax.random.fold_in(key, 71)
    key_scores, key_heavy, key_light = jax.random.split(base_key, 3)
    offsets = jnp.concatenate([jnp.arange(-SPAN, 0), jnp.arange(1, SPAN + 1)]).astype(jnp.int32)
    box_numbers = jnp.arange(BOXES).astype(jnp.int32)
    candidates = box_numbers[:, None] + offsets[None, :]
    in_range = (candidates >= 0) & (candidates < BOXES)
    positions = jnp.arange(2 * SPAN).astype(jnp.int32)[None, :]
    scores = jax.random.randint(key_scores, candidates.shape, 0, 1000) * 64 + positions
    scores = jnp.where(in_range, scores, -1 - positions)
    ranking = jnp.argsort(-scores, axis=1, stable=True)
    picked = jnp.take_along_axis(candidates, ranking, axis=1)[:, :MOST - 1]
    available = jnp.sum(in_range.astype(jnp.int32), axis=1) + 1
    heavy_device = jax.random.randint(key_heavy, (N_CLUSTER,), 0, 8) == 0
    heavy_device = heavy_device.at[N_CLUSTER // 2].set(True)
    heavy_box = jnp.repeat(heavy_device, LEAF_DEV)
    light_count = jax.random.randint(key_light, (BOXES,), 1, 4)
    near_counts = jnp.minimum(jnp.where(heavy_box, MOST, light_count), available).astype(jnp.int32)
    slot_numbers = jnp.arange(1, MOST)[None, :]
    rest = jnp.where(slot_numbers < near_counts[:, None], picked, box_numbers[:, None])
    identities = jnp.concatenate([box_numbers[:, None], rest], axis=1).astype(jnp.int32)
    return (identities, near_counts)


def draw_near_ids(key, part):
    return near_lists(key)[0]


def draw_near_count(key, part):
    return near_lists(key)[1]


def draw_leaf_pivots(key, part):
    box_keys = jax.random.split(jax.random.fold_in(key, 5), BOXES)
    shuffled = jax.vmap(lambda single: jax.random.permutation(single, LEAF))(box_keys)
    return shuffled[:, :RANK].astype(jnp.int32)


def draw_merge_pivots(key, part):
    pair_count = BOXES // 2
    box_keys = jax.random.split(jax.random.fold_in(key, 9), LEVELS * pair_count)
    shuffled = jax.vmap(lambda single: jax.random.permutation(single, 2 * RANK))(box_keys)
    shuffled = shuffled.reshape(LEVELS, pair_count, 2 * RANK)[:, :, :RANK]
    owner_rows = jnp.arange(pair_count)[:, None] // (2 ** jnp.arange(LEVELS))[None, :]
    level_numbers = jnp.arange(LEVELS)[None, :]
    return shuffled[level_numbers, owner_rows].astype(jnp.int32)


def levels(rng, dims, cuts, low, largest):
    loudness = 1.0
    for axis_at, blocks in cuts:
        heights = jax.random.uniform(jax.random.fold_in(jax.random.fold_in(rng, 6), axis_at), (blocks,), jnp.float32, low / len(cuts), largest / len(cuts))
        loudness = loudness * jnp.repeat(jnp.exp(heights), dims[axis_at] // blocks).reshape((-1,) + (1,) * (len(dims) - 1 - axis_at))
    return loudness


def normal_values(rng, extent, scale, bound, cuts=(), held_as=jnp.bfloat16):
    loudness = levels(rng, extent, cuts, -0.22, 0.18) if cuts else 1.0
    values = jax.random.normal(rng, extent, jnp.float32) * scale * loudness
    return jnp.minimum(jnp.maximum(values, -bound), bound).astype(held_as)


def setup_inputs(seed: int = 0) -> dict:
    seeds = jax.random.split(jax.random.key(seed), 7)
    points = draw_points(jax.random.fold_in(seeds[6], 71), 0)
    charges = normal_values(seeds[1], (BOXES, LEAF, R), 1.0, 6.0, ((0, 64), (1, 4)))
    near_ids = draw_near_ids(jax.random.fold_in(seeds[6], 71), 0)
    near_count = draw_near_count(jax.random.fold_in(seeds[6], 71), 0)
    leaf_pivots = draw_leaf_pivots(jax.random.fold_in(seeds[6], 71), 0)
    merge_pivots = draw_merge_pivots(jax.random.fold_in(seeds[6], 71), 0)
    return {"points": points, "charges": charges, "near_ids": near_ids, "near_count": near_count, "leaf_pivots": leaf_pivots, "merge_pivots": merge_pivots}


lengthscale = 0.7

def kernel_tile(left_set, right_set):
    left_wide = left_set.astype(jnp.float32)
    right_wide = right_set.astype(jnp.float32)
    squares = jnp.zeros((left_set.shape[1], right_set.shape[1]), jnp.float32)
    for feature in range(left_set.shape[0]):
        difference = left_wide[feature][:, None] - right_wide[feature][None, :]
        squares = squares + difference * difference
    return jnp.exp(-jnp.sqrt(squares) / lengthscale)

def merge_level(cand_coords, cand_weights, pivots):
    chosen = jnp.take(cand_coords, pivots, axis=1)
    tile_values = kernel_tile(chosen, cand_coords).astype(jnp.bfloat16)
    merged = jnp.dot(tile_values, cand_weights, preferred_element_type=jnp.float32).astype(jnp.bfloat16)
    return (chosen, merged)

def reference(points, charges, near_ids, near_count, leaf_pivots, merge_pivots):

    def near_one(box_index):
        own_coords = points[box_index]
        running = jnp.zeros((LEAF, R), jnp.float32)
        for slot_index in range(MOST):
            neighbour = near_ids[box_index, slot_index]
            live_slot = slot_index < near_count[box_index]
            neighbour_charges = jnp.where(live_slot, charges[neighbour], jnp.zeros((LEAF, R), charges.dtype))
            tile_values = kernel_tile(own_coords, points[neighbour]).astype(jnp.bfloat16)
            running = running + jnp.dot(tile_values, neighbour_charges, preferred_element_type=jnp.float32)
        return running.astype(jnp.bfloat16)
    near_field = lax.map(near_one, jnp.arange(BOXES).astype(jnp.int32))

    def apply_merge(operands):
        return merge_level(operands[0], operands[1], operands[2])
    coords, weights = lax.map(apply_merge, (points, charges, leaf_pivots))
    for level_index in range(LEVELS):
        stride = 2 ** level_index
        cand_coords = jnp.concatenate([coords[0::2], coords[1::2]], axis=2)
        cand_weights = jnp.concatenate([weights[0::2], weights[1::2]], axis=1)
        level_pivots = merge_pivots[0::stride, level_index]
        coords, weights = lax.map(apply_merge, (cand_coords, cand_weights, level_pivots))
    top_weights = jnp.repeat(weights, 2 ** LEVELS // LEAF_DEV, axis=0)
    return (near_field, top_weights)
```

```python
import functools

import jax
import jax.numpy as jnp
from jax import lax
from jax.experimental import pallas as pl
from jax.experimental.pallas import tpu as pltpu
from jax.sharding import PartitionSpec as P

MESH = pl.DeviceIdType.MESH
F32 = jnp.float32
BF16 = jnp.bfloat16

SPAN = 4
MOST = 8
BOXES = 8
WIN = BOXES + 2 * SPAN
ROWS = 128
LEAF = 512
RANK = 256
R = 256
HALF = 128
LOCAL = 15
CROSS = 3
DEPTH = 128

SCALE = 1.4426950408889634 / 0.7
LIMIT = 1e17
FAR = float(2**20)


def split(raw, centre):
    u = jnp.clip((raw - centre) * SCALE, -LIMIT, LIMIT)
    hi = u.astype(BF16).astype(F32)
    lo = (u - hi).astype(BF16).astype(F32)
    both = hi + lo
    norm = jnp.sum(both * both, axis=0, keepdims=True)
    n1 = norm.astype(BF16).astype(F32)
    n2 = (norm - n1).astype(BF16).astype(F32)
    n3 = (norm - n1 - n2).astype(BF16).astype(F32)
    return hi, lo, (n1, n2, n3)


def by_row(values, shape):
    row = lax.broadcasted_iota(jnp.int32, shape, 0)
    out = jnp.zeros(shape, F32)
    for at, value in enumerate(values):
        if value is not None:
            out = jnp.where(row == at, value, out)
    return out


def left_rows(hi, lo, norms, extra=None):
    n = hi.shape[1]
    parts = [-2.0 * hi, -2.0 * hi, -2.0 * lo, -2.0 * lo]
    parts.append(by_row(list(norms) + [1.0] * 3, (8, n)))
    used = 40
    if extra is not None:
        parts.append(extra)
        used += extra.shape[0]
    parts.append(jnp.zeros((DEPTH - used, n), F32))
    return jnp.concatenate(parts, axis=0)


def right_rows(hi, lo, norms, extra=None):
    n = hi.shape[1]
    parts = [hi, lo, hi, lo]
    parts.append(by_row([1.0] * 3 + list(norms), (8, n)))
    used = 40
    if extra is not None:
        parts.append(extra)
        used += extra.shape[0]
    parts.append(jnp.zeros((DEPTH - used, n), F32))
    return jnp.concatenate(parts, axis=0)


def decay(squares):
    floor = jnp.maximum(squares, 1e-12)
    return jnp.exp2(-(floor * lax.rsqrt(floor)))


def mm(a, b):
    return jnp.dot(a, b, preferred_element_type=F32)


def mm_t(a, b):
    return lax.dot_general(a, b, (((1,), (1,)), ((), ())), preferred_element_type=F32)


def kernel(
    C, T, ids_ref, count_ref, points_ref, charges_ref, leaf_ref, merge_ref, near_ref, top_ref,
    q, pw, left, right, k_own, k_halo, k_tree, cand, piv, xc, xw, wc, acc,
    s_pt, r_pt, s_a, r_a, s_f, r_f, s_h, r_h, s_xc, r_xc, s_xw, r_xw, s_own,
):
    c = lax.axis_index("cluster")
    t = lax.axis_index("tile")
    up, down = lax.rem(c + 1, C), lax.rem(c + C - 1, C)

    def tile_at(k):
        return lax.rem(t + k, T)

    bits = [lax.rem(c // (1 << i), 2) for i in range(CROSS)]
    mates = [c + (1 << i) * (1 - 2 * bits[i]) for i in range(CROSS)]

    barrier = pltpu.get_barrier_semaphore()
    greeted = [(c, tile_at(k)) for k in range(1, T)]
    greeted += [(cc, tile_at(k)) for cc in (up, down) for k in range(T)]
    greeted += [(mates[i], t) for i in range(1, CROSS)]
    for device in greeted:
        pl.semaphore_signal(barrier, inc=1, device_id=device, device_id_type=MESH)
    pl.semaphore_wait(barrier, len(greeted))

    sent = []

    def send(src, dst, send_sem, recv_sem, device):
        copy = pltpu.make_async_remote_copy(
            src_ref=src, dst_ref=dst, send_sem=send_sem, recv_sem=recv_sem,
            device_id=device, device_id_type=MESH,
        )
        copy.start()
        sent.append(copy)

    def arrived(dst, recv_sem):
        pltpu.make_async_remote_copy(
            src_ref=dst, dst_ref=dst, send_sem=s_own, recv_sem=recv_sem,
            device_id=(c, tile_at(1)), device_id_type=MESH,
        ).wait_recv()

    def lanes(s):
        return pl.ds(pl.multiple_of(s * ROWS, ROWS), ROWS)

    for k in range(1, T):
        send(points_ref, pw.at[pl.ds(SPAN, BOXES), :, lanes(t)], s_pt.at[k - 1], r_pt.at[k - 1], (c, tile_at(k)))
    for k in range(T):
        send(points_ref.at[pl.ds(BOXES - SPAN, SPAN)], pw.at[pl.ds(0, SPAN), :, lanes(t)],
             s_pt.at[3 + k], r_pt.at[3 + t], (up, tile_at(k)))
        send(points_ref.at[pl.ds(0, SPAN)], pw.at[pl.ds(SPAN + BOXES, SPAN), :, lanes(t)],
             s_pt.at[7 + k], r_pt.at[7 + t], (down, tile_at(k)))

    odd = lax.rem(c, 2)
    base = [SPAN * odd, SPAN - SPAN * odd]
    side = [odd, 1 - odd]
    over = [jnp.where(odd == 1, up, down), jnp.where(odd == 1, down, up)]

    def rows(s, at=0, n=ROWS):
        return pl.ds(pl.multiple_of(s * ROWS + at, 64), n)

    def place(g, s, at=0, n=ROWS):
        return q.at[pl.ds(SPAN + base[g], SPAN), rows(s, at, n)]

    def onward(g, s, piece, src=None, at=0, n=ROWS):
        there = pl.ds((SPAN + BOXES) * (1 - side[g]), SPAN)
        send(place(g, s, at, n) if src is None else src, q.at[there, rows(s, at, n)],
             s_h.at[g, piece], r_h.at[side[g], piece], (over[g], t))

    own = pltpu.make_async_copy(charges_ref, q.at[pl.ds(SPAN, BOXES), rows(t)], s_own)
    own.start()
    for g in range(2):
        mine = charges_ref.at[pl.ds(base[g], SPAN)]
        send(mine, place(g, t), s_a.at[g, 0], r_a.at[g, 0], (c, tile_at(1)))
        send(mine, place(g, t), s_a.at[g, 1], r_a.at[g, 1], (c, tile_at(T - 1)))
        onward(g, t, 0, mine)

    def forward(g):
        before, after = tile_at(T - 1), tile_at(1)
        arrived(place(g, before), r_a.at[g, 0])
        send(place(g, before, 0, 64), place(g, before, 0, 64), s_f.at[g, 0], r_f.at[g, 0], (c, after))
        onward(g, before, 1)
        arrived(place(g, after), r_a.at[g, 1])
        send(place(g, after, 64, 64), place(g, after, 64, 64), s_f.at[g, 1], r_f.at[g, 1], (c, before))
        onward(g, after, 2)

    def finish(g):
        across = tile_at(2)
        arrived(place(g, across, 0, 64), r_f.at[g, 0])
        onward(g, across, 3, None, 0, 64)
        arrived(place(g, across, 64, 64), r_f.at[g, 1])
        onward(g, across, 4, None, 64, 64)

    def halo_arrived(which):
        there = pl.ds((SPAN + BOXES) * (1 - which), SPAN)
        arrived(q.at[there, rows(t)], r_h.at[which, 0])
        arrived(q.at[there, rows(tile_at(T - 1))], r_h.at[which, 1])
        arrived(q.at[there, rows(tile_at(1))], r_h.at[which, 2])
        arrived(q.at[there, rows(tile_at(2), 0, 64)], r_h.at[which, 3])
        arrived(q.at[there, rows(tile_at(2), 64, 64)], r_h.at[which, 4])

    pw[pl.ds(SPAN, BOXES), :, lanes(t)] = points_ref[...]
    piv[pl.ds(0, BOXES), :] = leaf_ref[...]
    for m, (q_at, level) in enumerate(
        [(0, 0), (1, 0), (2, 0), (3, 0), (0, 1), (2, 1), (0, 2), (0, 3), (0, 4), (0, 5)]
    ):
        piv[pl.ds(BOXES + m, 1), :] = merge_ref[q_at, pl.ds(level, 1), :]
    none = jnp.zeros((ROWS, LEAF), BF16)
    for b in range(BOXES):
        for w in range(WIN):
            if not b <= w <= b + 2 * SPAN:
                if SPAN <= w < SPAN + BOXES:
                    k_own[w - SPAN, pl.ds(b * ROWS, ROWS), :] = none
                elif w < SPAN and b < SPAN:
                    k_halo[w, pl.ds(b * ROWS, ROWS), :] = none
                elif w >= SPAN + BOXES and b >= SPAN:
                    k_halo[w - BOXES, pl.ds((b - SPAN) * ROWS, ROWS), :] = none

    centre = points_ref[BOXES // 2].astype(F32)[:, 0:1]
    first = c * BOXES - SPAN
    slot = lax.broadcasted_iota(jnp.int32, (WIN, ROWS), 0)

    for b in range(BOXES):
        used = jnp.zeros((WIN, ROWS), jnp.bool_)
        for j in range(MOST):
            at = jnp.where(j < count_ref[b], ids_ref[b, j] - first, -1)
            used = used | (slot == at)
        hi, lo, norms = split(points_ref[b].astype(F32), centre)
        stack = left_rows(hi, lo, norms, jnp.where(used, 0.0, FAR))
        left[b] = stack.T.astype(BF16)

    for k in range(1, T):
        arrived(pw.at[pl.ds(SPAN, BOXES), :, lanes(tile_at(T - k))], r_pt.at[k - 1])
    for s in range(T):
        arrived(pw.at[pl.ds(0, SPAN), :, lanes(s)], r_pt.at[3 + s])
        arrived(pw.at[pl.ds(SPAN + BOXES, SPAN), :, lanes(s)], r_pt.at[7 + s])

    cand[pl.ds(0, BOXES)] = pw[pl.ds(SPAN, BOXES)]

    def right_of(w, carry):
        hi, lo, norms = split(pw[w].astype(F32), centre)
        hot = jnp.where(lax.broadcasted_iota(jnp.int32, (WIN, LEAF), 0) == w, 1.0, 0.0)
        right[w] = right_rows(hi, lo, norms, hot).astype(BF16)
        return carry

    lax.fori_loop(0, WIN, right_of, 0)

    lane = lax.broadcasted_iota(jnp.int32, (ROWS, LEAF), 1)
    row = lax.broadcasted_iota(jnp.int32, (ROWS, LEAF), 0)

    def tile(b, w):
        return decay(mm(left[b], right[w]))

    for b in range(BOXES):
        for w in range(b, b + 2 * SPAN + 1):
            value = tile(b, w)
            if w == b + SPAN:
                value = jnp.where(lane == row + t * ROWS, 1.0, value)
            value = value.astype(BF16)
            if SPAN <= w < SPAN + BOXES:
                k_own[w - SPAN, pl.ds(b * ROWS, ROWS), :] = value
            elif w < SPAN:
                k_halo[w, pl.ds(b * ROWS, ROWS), :] = value
            else:
                k_halo[w - BOXES, pl.ds((b - SPAN) * ROWS, ROWS), :] = value

    forward(0)

    column = lax.broadcasted_iota(jnp.int32, (RANK, LEAF), 1).astype(F32)

    def merge(m, raw):
        wide = raw.astype(F32)
        hi, lo, norms = split(wide, wide[:, 0:1])
        chosen = jnp.broadcast_to(piv[pl.ds(m, 1), :].astype(F32), (HALF, RANK)).T
        picked = jnp.concatenate([chosen] * (LEAF // HALF), axis=1) == column
        hot = jnp.where(picked, 1.0, 0.0).astype(BF16)
        skel = mm_t(hot, left_rows(hi, lo, norms).astype(BF16)).astype(BF16)
        value = decay(mm(skel, right_rows(hi, lo, norms).astype(BF16)))
        k_tree[m] = jnp.where(picked, 1.0, value).astype(BF16)
        return mm_t(raw, hot).astype(BF16)

    def local_merge(m, carry):
        at = pl.multiple_of(lax.rem(m, 2) * RANK, RANK)
        cand[BOXES + m // 2, :, pl.ds(at, RANK)] = merge(m, cand[m])
        return carry

    lax.fori_loop(0, LOCAL - 1, local_merge, 0)
    skel = merge(LOCAL - 1, cand[LOCAL - 1])

    def swap(x, s_x, r_x, i, value):
        x[i, bits[i]] = value
        send(x.at[i, bits[i]], x.at[i, bits[i]], s_x.at[i], r_x.at[i], (mates[i], t))

    def swapped(x, r_x, i):
        arrived(x.at[i, 1 - bits[i]], r_x.at[i])

    swap(xc, s_xc, r_xc, 0, skel)
    forward(1)
    for i in range(CROSS):
        swapped(xc, r_xc, i)
        skel = merge(LOCAL + i, jnp.concatenate([xc[i, 0], xc[i, 1]], axis=1))
        if i + 1 < CROSS:
            swap(xc, s_xc, r_xc, i + 1, skel)
    finish(0)
    finish(1)
    own.wait()

    half = pl.ds(pl.multiple_of(t // 2 * HALF, HALF), HALF)
    for m in range(LOCAL):
        below = q[SPAN + m, :, half] if m < BOXES else wc[m - BOXES]
        weights = mm(k_tree[m], below).astype(BF16)
        if m + 1 < LOCAL:
            wc[m // 2, pl.ds(m % 2 * RANK, RANK), :] = weights
    swap(xw, s_xw, r_xw, 0, weights)

    def near_own(w, carry):
        acc[...] += mm(k_own[w], q[SPAN + w])
        return carry

    acc[...] = mm(k_own[0], q[SPAN])
    parts = [(1, 4), (4, 8)]
    for i in range(CROSS):
        if i < len(parts):
            lax.fori_loop(parts[i][0], parts[i][1], near_own, 0)
        else:
            for which in (1, 0):
                halo_arrived(which)
                r0 = 0 if which == 1 else BOXES // 2 * ROWS

                def near_halo(w, carry):
                    at = w if which == 1 else w + SPAN
                    source = w if which == 1 else w + SPAN + BOXES
                    acc[pl.ds(r0, BOXES // 2 * ROWS), :] += mm(k_halo[at], q[source])
                    return carry

                lax.fori_loop(0, SPAN, near_halo, 0)
        swapped(xw, r_xw, i)
        weights = mm(k_tree[LOCAL + i, :, pl.ds(0, RANK)], xw[i, 0])
        weights += mm(k_tree[LOCAL + i, :, pl.ds(RANK, RANK)], xw[i, 1])
        if i + 1 < CROSS:
            swap(xw, s_xw, r_xw, i + 1, weights.astype(BF16))
    mine = jnp.where(lax.rem(t, 2) == 1, pltpu.roll(weights, HALF // 2, 1), weights)
    top_ref[0] = mine[:, : HALF // 2].astype(BF16)
    for b in range(BOXES):
        near_ref[b] = acc[pl.ds(b * ROWS, ROWS), :].astype(BF16)
    for copy in sent:
        copy.wait_send()


def solution(mesh):
    C, T = mesh.shape["cluster"], mesh.shape["tile"]

    def on_device(points, charges, near_ids, near_count, leaf_pivots, merge_pivots):
        vmem = pl.BlockSpec(memory_space=pltpu.VMEM)
        smem = pl.BlockSpec(memory_space=pltpu.SMEM)
        dma = pltpu.SemaphoreType.DMA
        return pl.pallas_call(
            functools.partial(kernel, C, T),
            out_shape=(
                jax.ShapeDtypeStruct((BOXES, ROWS, R), BF16),
                jax.ShapeDtypeStruct((1, RANK, HALF // 2), BF16),
            ),
            in_specs=[smem, smem, vmem, vmem, vmem, vmem],
            out_specs=(vmem, vmem),
            scratch_shapes=[
                pltpu.VMEM((WIN, LEAF, R), BF16),
                pltpu.VMEM((WIN, 8, LEAF), BF16),
                pltpu.VMEM((BOXES, ROWS, DEPTH), BF16),
                pltpu.VMEM((WIN, DEPTH, LEAF), BF16),
                pltpu.VMEM((BOXES, BOXES * ROWS, LEAF), BF16),
                pltpu.VMEM((2 * SPAN, SPAN * ROWS, LEAF), BF16),
                pltpu.VMEM((LOCAL + CROSS, RANK, LEAF), BF16),
                pltpu.VMEM((LOCAL, 8, LEAF), BF16),
                pltpu.VMEM((LOCAL + CROSS, RANK), jnp.int32),
                pltpu.VMEM((CROSS, 2, 8, RANK), BF16),
                pltpu.VMEM((CROSS, 2, RANK, HALF), BF16),
                pltpu.VMEM((LOCAL - BOXES, LEAF, HALF), BF16),
                pltpu.VMEM((BOXES * ROWS, R), F32),
                dma((11,)), dma((11,)), dma((2, 2)), dma((2, 2)), dma((2, 2)), dma((2, 2)),
                dma((2, 5)), dma((2, 5)), dma((CROSS,)), dma((CROSS,)), dma((CROSS,)), dma((CROSS,)),
                dma(()),
            ],
            compiler_params=pltpu.CompilerParams(
                collective_id=0, has_side_effects=True, vmem_limit_bytes=56 * 2**20
            ),
        )(near_ids, near_count, points, charges, leaf_pivots, merge_pivots)

    return jax.shard_map(
        on_device,
        mesh=mesh,
        in_specs=(
            P("cluster", None, "tile"),
            P("cluster", "tile", None),
            P("cluster", None),
            P("cluster"),
            P("cluster", None),
            P("cluster", None, None),
        ),
        out_specs=(P("cluster", "tile", None), P("cluster", None, "tile")),
        check_vma=False,
    )
```
